1024 devices in a mesh: outer: 32 (over z, x_lo), inner: 16 (over y, core), chan: 2 (over x_hi).
Axes of the slice: x: 4 (x_hi: 2, x_lo: 2; x = x_hi * 2 + x_lo), y: 8, z: 16, core: 2. Of those that a mesh axis runs over, the one named last changes fastest.
Arguments:
- query_in: bfloat16 [256, 131072], P('chan', ('outer', 'inner')), may hold values from -6 to 6
- key_in: bfloat16 [256, 131072], P('chan', ('outer', 'inner')), may hold values from -6 to 6
- value_in: bfloat16 [256, 131072], P('chan', ('outer', 'inner')), may hold values from -6 to 6
- short_filter: float32 [256, 128], P('chan'), may hold values from -2 to 2
- tap_counts: int32 [16], replicated, may hold values from 1 to 128, as said below
- long_filter: float32 [256, 131072], P('chan', ('outer', 'inner')), may hold values from -0.015625 to 0.015625
- skip_gain: float32 [256], P('chan'), may hold values from -6 to 6
Outputs:
- mixed_out: bfloat16 [256, 131072], P('chan', ('outer', 'inner'))
The draws below stay inside these ranges and needn't reach their ends.
Inputs may be any that keep to these rules, and one draw needn't show every extreme that they name: tap_counts[g] is how many leading taps channel group g uses; some group uses all 128 taps and some group uses only tap 0.
All inputs are finite; a program needn't handle non-finite values.
Results may differ from the reference program's by a relative error of at most 0.0065.
Values may be sent and summed in bfloat16 or wider, within the bound.
A program may use at most 32 MiB of HBM per device.

```python
import jax
import jax.numpy as jnp
from jax import lax

TAPS = 128
GROUP_CH = 16
SEQ = 131072
CH = 256
GROUPS = 16


def draw_tap_counts(key, part):
    first_key = jax.random.fold_in(key, 11)
    second_key = jax.random.fold_in(key, 12)
    counts = jax.random.randint(first_key, (GROUPS,), 1, TAPS + 1, dtype=jnp.int32)
    shuffled = jax.random.permutation(second_key, GROUPS)
    counts = counts.at[shuffled[0]].set(TAPS)
    counts = counts.at[shuffled[1]].set(1)
    return counts


def block_levels(own_key, extent, cuts, low, high):
    def one(axis_at, shards_of):
        draws = jax.random.uniform(jax.random.fold_in(jax.random.fold_in(own_key, 6), axis_at), (shards_of,), jnp.float32, low / len(cuts), high / len(cuts))
        return jnp.repeat(jnp.exp(draws), extent[axis_at] // shards_of).reshape((-1,) + (1,) * (len(extent) - axis_at - 1))

    gain = one(*cuts[0])
    for cut in cuts[1:]:
        gain = gain * one(*cut)
    return gain


def noise(own_key, shape, width, limit, cuts=(), kind=jnp.bfloat16):
    values = width * jax.random.normal(own_key, shape, jnp.float32)
    if cuts:
        values = values * block_levels(own_key, shape, cuts, -0.22, 0.18)
    return jnp.clip(values, -limit, limit).astype(kind)


def setup_inputs(seed: int = 0) -> dict:
    key_of = jax.random.split(jax.random.key(seed), 8)
    query_in = noise(key_of[0], (CH, SEQ), 1.0, 6.0, ((0, 2), (1, 512)))
    key_in = noise(key_of[1], (CH, SEQ), 1.0, 6.0, ((0, 2), (1, 512)))
    value_in = noise(key_of[2], (CH, SEQ), 1.0, 6.0, ((0, 2), (1, 512)))
    short_filter = noise(key_of[3], (CH, TAPS), 0.15, 2.0, ((0, 2),), jnp.float32)
    tap_counts = draw_tap_counts(jax.random.fold_in(key_of[7], 71), 0)
    long_filter = noise(key_of[5], (CH, SEQ), SEQ ** -0.5, 0.015625, ((0, 2), (1, 512)), jnp.float32)
    skip_gain = noise(key_of[6], (CH,), 1.0, 6.0, ((0, 2),), jnp.float32)
    return dict(query_in=query_in, key_in=key_in, value_in=value_in, short_filter=short_filter, tap_counts=tap_counts, long_filter=long_filter, skip_gain=skip_gain)


def one_group(items):
    query_in, key_in, value_in, taps_kept, long_filter, skip_gain = items
    total_len = 2 * SEQ
    values_f = value_in.astype(jnp.float32)
    short_out = jnp.fft.irfft(jnp.fft.rfft(values_f, n=total_len, axis=1) * jnp.fft.rfft(taps_kept, n=total_len, axis=1), n=total_len, axis=1)[:, :SEQ]
    gated_in = key_in.astype(jnp.float32) * short_out
    long_out = jnp.fft.irfft(jnp.fft.rfft(gated_in, n=total_len, axis=1) * jnp.fft.rfft(long_filter, n=total_len, axis=1), n=total_len, axis=1)[:, :SEQ]
    mixed_out = query_in.astype(jnp.float32) * (long_out + skip_gain[:, None] * gated_in)
    return mixed_out.astype(jnp.bfloat16)


def by_group(array):
    return array.reshape((GROUPS, GROUP_CH) + array.shape[1:])


def reference(query_in, key_in, value_in, short_filter, tap_counts, long_filter, skip_gain):
    group_ids = jnp.arange(CH, dtype=jnp.int32) // GROUP_CH
    counts = tap_counts[group_ids]
    live_taps = jnp.arange(TAPS, dtype=jnp.int32)[None, :] < counts[:, None]
    taps_kept = jnp.where(live_taps, short_filter, jnp.zeros_like(short_filter))
    result = lax.map(one_group, (by_group(query_in), by_group(key_in), by_group(value_in), by_group(taps_kept), by_group(long_filter), by_group(skip_gain)))
    return result.reshape(CH, SEQ)
```

```python
import functools
import math

import jax
import jax.numpy as jnp
import numpy as np
from jax import lax
from jax.experimental import pallas as pl
from jax.experimental.pallas import tpu as pltpu
from jax.sharding import PartitionSpec as P

GROUP_CH = 16
LANES = 128
CHANNELS = 128
LENGTH = 256
ROWS = 256
MESH = pl.DeviceIdType.MESH
f32 = jnp.float32
bf16 = jnp.bfloat16


def split_np(table):
    high = table.astype(bf16)
    low = (table - high.astype(np.float64)).astype(bf16)
    return high, low


def fine_tables(outer_count, inner_count):
    set_ch = CHANNELS // outer_count
    local = outer_count // inner_count
    fine = 2 * inner_count
    pos = np.arange(fine).reshape(inner_count, 2)
    freq = np.arange(fine)
    angle = 2.0 * np.pi / fine * (freq[:, None, None] * pos[None] % fine)
    cos, sin = np.cos(angle), np.sin(angle)
    table = np.zeros((2, fine, local, set_ch, inner_count, local, 2, set_ch, 2))
    for one in range(local):
        for chan in range(set_ch):
            table[0, :, one, chan, :, one, 0, chan, :] = cos
            table[0, :, one, chan, :, one, 1, chan, :] = sin
            table[1, :, one, chan, :, one, 0, chan, :] = -sin
            table[1, :, one, chan, :, one, 1, chan, :] = cos
    fine_tab = table.reshape(2 * ROWS, 2 * ROWS)
    steps = np.arange(LANES)
    angle = 2.0 * np.pi / LANES * (steps[:, None] * steps[None] % LANES)
    cos, sin = np.cos(angle), np.sin(angle)
    lane_tab = np.block([[cos, -sin], [sin, cos]])
    fine_all = np.stack([*split_np(fine_tab), *split_np(fine_tab.T)])
    lane_all = np.stack([*split_np(lane_tab), *split_np(lane_tab.T)])
    return fine_all, lane_all


def cos_turns(steps, period):
    half = period // 2
    centred = ((steps + half) & (period - 1)) - half
    x = centred.astype(f32) * (math.pi / period)
    y = x * x
    tail = y * (-1.0 / 5040 + y * (1.0 / 362880 - y * (1.0 / 39916800)))
    s = x * (1.0 + y * (-1.0 / 6 + y * (1.0 / 120 + tail)))
    return 1.0 - 2.0 * s * s


def split(value):
    high = value.astype(bf16)
    return high, (value - high.astype(f32)).astype(bf16)


def dot(left, right):
    return jnp.dot(left, right, preferred_element_type=f32)


def iota2(shape, dim):
    return lax.broadcasted_iota(jnp.int32, shape, dim)


def kernel(
    sizes, query_hbm, key_hbm, value_hbm, taps_hbm, filter_hbm, fine_hbm, lane_hbm, counts_ref, skip_ref,
    out_ref,
    query_ref, key_ref, value_ref, taps_ref, filter_ref, fine_ref, lane_ref,
    edge_ref, window_ref, kept_ref, coarse_ref, back_ref,
    send_h, send_g, send_y, recv_h, recv_g, recv_y,
    mid_send_h, mid_send_g, mid_send_y, mid_recv_h, mid_recv_g, mid_recv_y,
    load_sem, send_sem, recv_sem,
):
    outer_count, inner_count = sizes
    set_ch = CHANNELS // outer_count
    rows = 2 * set_ch
    local = outer_count // inner_count
    fine = 2 * inner_count
    total = outer_count * inner_count * LENGTH
    outer_pos, inner_pos = lax.axis_index("outer"), lax.axis_index("inner")
    block_pos = outer_pos * inner_count + inner_pos
    blocks = outer_count * inner_count

    def block_id(pos):
        return {"outer": pos // inner_count, "inner": lax.rem(pos, inner_count)}

    following = block_id(lax.rem(block_pos + 1, blocks))
    preceding = block_id(lax.rem(block_pos + blocks - 1, blocks))

    def far_first(step, count):
        offset = count // 2 + (1 - 2 * lax.rem(step, 2)) * ((step + 1) // 2)
        return offset

    def outer_peer(step):
        return lax.rem(outer_pos + far_first(step, outer_count), outer_count)

    def inner_peer(step):
        return lax.rem(inner_pos + far_first(step, inner_count), inner_count)

    barrier = pltpu.get_barrier_semaphore()

    def greet_outer(step, carry):
        pl.semaphore_signal(barrier, inc=1, device_id={"outer": outer_peer(step)}, device_id_type=MESH)
        return carry

    def greet_inner(step, carry):
        pl.semaphore_signal(barrier, inc=1, device_id={"inner": inner_peer(step)}, device_id_type=MESH)
        return carry

    lax.fori_loop(0, outer_count - 1, greet_outer, 0)
    lax.fori_loop(0, inner_count - 1, greet_inner, 0)
    pl.semaphore_signal(barrier, inc=1, device_id=following, device_id_type=MESH)
    pl.semaphore_signal(barrier, inc=1, device_id=preceding, device_id_type=MESH)

    loads = [
        pltpu.make_async_copy(source, target, load_sem.at[place])
        for place, (source, target) in enumerate(
            [
                (value_hbm, value_ref), (taps_hbm, taps_ref), (filter_hbm, filter_ref),
                (key_hbm, key_ref), (query_hbm, query_ref), (fine_hbm, fine_ref), (lane_hbm, lane_ref),
            ]
        )
    ]
    for load in loads:
        load.start()

    row = iota2((ROWS, ROWS), 0)
    col = iota2((ROWS, ROWS), 1)
    spread = jnp.where(col == (row & 1) * LANES + (row >> 1), 1.0, 0.0).astype(bf16)

    def to_sets(value):
        halves = jnp.concatenate([value[:, :LANES], value[:, LANES:]], axis=0).astype(bf16)
        return dot(spread, halves).reshape(outer_count, rows, LANES).astype(bf16)

    def from_sets(ref):
        return ref[...].astype(f32).reshape(ROWS, LANES).astype(bf16)

    def exchange_outer(send_ref, recv_ref, place):
        def one(step, carry):
            peer = outer_peer(step)
            pltpu.make_async_remote_copy(
                src_ref=send_ref.at[peer], dst_ref=recv_ref.at[outer_pos],
                send_sem=send_sem.at[place], recv_sem=recv_sem.at[place],
                device_id={"outer": peer}, device_id_type=MESH,
            ).start()
            return carry

        lax.fori_loop(0, outer_count - 1, one, 0)
        pltpu.make_async_copy(send_ref.at[outer_pos], recv_ref.at[outer_pos], recv_sem.at[place]).start()

    def exchange_inner(send_ref, recv_ref, place):
        def one(step, carry):
            peer = inner_peer(step)
            pltpu.make_async_remote_copy(
                src_ref=send_ref.at[peer], dst_ref=recv_ref.at[inner_pos],
                send_sem=send_sem.at[place], recv_sem=recv_sem.at[place],
                device_id={"inner": peer}, device_id_type=MESH,
            ).start()
            return carry

        lax.fori_loop(0, inner_count - 1, one, 0)
        pltpu.make_async_copy(send_ref.at[inner_pos], recv_ref.at[inner_pos], recv_sem.at[place]).start()

    def arrived(recv_ref, place):
        pltpu.make_async_copy(recv_ref, recv_ref, recv_sem.at[place]).wait()

    def sent(send_ref, place):
        part = send_ref.at[pl.ds(0, send_ref.shape[0] - 1)]
        pltpu.make_async_copy(part, part, send_sem.at[place]).wait()

    loads[1].wait()
    lane = iota2((1, LANES), 1)
    counts = jnp.zeros((1, LANES), jnp.int32)
    first_group = lax.axis_index("chan") * (CHANNELS // GROUP_CH)
    for group in range(CHANNELS // GROUP_CH):
        counts = jnp.where(lane // GROUP_CH == group, counts_ref[first_group + group], counts)
    live = iota2((LANES, CHANNELS), 0) < counts
    kept_ref[...] = jnp.where(live, jnp.transpose(taps_ref[...]), 0.0)

    def short_filter(start):
        def eight(step, acc):
            for one in range(8):
                tap = step * 8 + one
                acc = acc + kept_ref[pl.ds(tap, 1), :] * window_ref[pl.ds(start + LANES - tap, LANES), :]
            return acc

        return lax.fori_loop(0, LANES // 8, eight, jnp.zeros((LANES, CHANNELS), f32))

    loads[0].wait()
    window_ref[LANES:, :] = jnp.transpose(value_ref[...].astype(f32))
    short_late = jnp.transpose(short_filter(LANES))

    loads[2].wait()
    send_h[...] = to_sets(filter_ref[...])

    period = 4 * outer_count * fine

    def coarse_table(freq_dim):
        shape = (2 * ROWS, ROWS) if freq_dim == 0 else (ROWS, 2 * ROWS)
        place = iota2(shape, freq_dim)
        token = iota2(shape, 1 - freq_dim)
        freq = place // (2 * rows)
        imag = (place // rows) & 1
        step = (token // rows) * fine + 2 * inner_pos + (token & 1)
        value = cos_turns((4 * freq + 1) * step + imag * (period // 4), period)
        return jnp.where((place & (rows - 1)) == (token & (rows - 1)), value, 0.0)

    coarse_ref[0], coarse_ref[1] = split(coarse_table(0))

    pl.semaphore_wait(barrier, outer_count + inner_count)
    edge = pltpu.make_async_remote_copy(
        src_ref=value_ref.at[:, pl.ds(LANES, LANES)], dst_ref=edge_ref,
        send_sem=send_sem.at[6], recv_sem=recv_sem.at[6],
        device_id=following, device_id_type=MESH,
    )
    edge.start()
    exchange_outer(send_h, recv_h, 0)

    loads[3].wait()
    edge.wait_recv()
    before = jnp.transpose(edge_ref[...].astype(f32))
    window_ref[:LANES, :] = jnp.where(block_pos == 0, jnp.zeros_like(before), before)
    short_early = jnp.transpose(short_filter(0))
    gated = key_ref[...].astype(f32) * jnp.concatenate([short_early, short_late], axis=1)
    send_g[...] = to_sets(gated)
    exchange_outer(send_g, recv_g, 1)

    back_ref[0], back_ref[1] = split(coarse_table(1))
    place = iota2((ROWS, LANES), 0)
    near = iota2((ROWS, LANES), 1)
    freq = inner_pos * local + ((place // set_ch) & (local - 1))
    turn = (4 * freq + 1 + 4 * outer_count * (place // (set_ch * local))) * near
    twist_cos = cos_turns(turn, 4 * total)
    twist_sin = cos_turns(turn + 3 * total, 4 * total)
    skip_eye = iota2((CHANNELS, CHANNELS), 0) == iota2((CHANNELS, CHANNELS), 1)
    skip_col = jnp.sum(jnp.where(skip_eye, skip_ref[...], 0.0), axis=1, keepdims=True)
    skipped = skip_col * gated
    loads[4].wait()
    loads[5].wait()
    loads[6].wait()

    def coarse_forward(recv_ref, send_ref):
        block = from_sets(recv_ref)
        value = dot(coarse_ref[0], block) + dot(coarse_ref[1], block)
        send_ref[...] = value.astype(bf16).reshape(inner_count, 2 * local * rows, LANES)

    def fine_forward(recv_ref):
        block = recv_ref[...].reshape(2 * ROWS, LANES)
        value = dot(fine_ref[0], block) + dot(fine_ref[1], block)
        real, imag = value[:ROWS], value[ROWS:]
        turned = jnp.concatenate(
            [real * twist_cos + imag * twist_sin, imag * twist_cos - real * twist_sin], axis=1
        )
        high, low = split(turned)
        return dot(high, lane_ref[0]) + dot(low, lane_ref[0]) + dot(high, lane_ref[1])

    arrived(recv_h, 0)
    coarse_forward(recv_h, mid_send_h)
    exchange_inner(mid_send_h, mid_recv_h, 2)
    arrived(recv_g, 1)
    coarse_forward(recv_g, mid_send_g)
    exchange_inner(mid_send_g, mid_recv_g, 3)

    arrived(mid_recv_h, 2)
    spec_h = fine_forward(mid_recv_h) * (1.0 / total)
    arrived(mid_recv_g, 3)
    spec_g = fine_forward(mid_recv_g)

    h_real, h_imag = spec_h[:, :LANES], spec_h[:, LANES:]
    g_real, g_imag = spec_g[:, :LANES], spec_g[:, LANES:]
    product = jnp.concatenate(
        [g_real * h_real - g_imag * h_imag, g_real * h_imag + g_imag * h_real], axis=1
    )
    high, low = split(product)
    value = dot(high, lane_ref[2]) + dot(low, lane_ref[2]) + dot(high, lane_ref[3])
    real, imag = value[:, :LANES], value[:, LANES:]
    turned = jnp.concatenate(
        [real * twist_cos - imag * twist_sin, imag * twist_cos + real * twist_sin], axis=0
    )
    high, low = split(turned)
    value = dot(fine_ref[2], high) + dot(fine_ref[2], low) + dot(fine_ref[3], high)
    mid_send_y[...] = value.astype(bf16).reshape(inner_count, 2 * local * rows, LANES)
    exchange_inner(mid_send_y, mid_recv_y, 4)

    gather = jnp.where(row == (col & 1) * LANES + (col >> 1), 1.0, 0.0).astype(bf16)
    arrived(mid_recv_y, 4)
    block = mid_recv_y[...].reshape(2 * ROWS, LANES)
    value = dot(back_ref[0], block) + dot(back_ref[1], block)
    send_y[...] = value.reshape(outer_count, rows, LANES).astype(bf16)
    exchange_outer(send_y, recv_y, 5)

    arrived(recv_y, 5)
    halves = dot(gather, from_sets(recv_y))
    long_out = jnp.concatenate([halves[:LANES], halves[LANES:]], axis=1)
    out_ref[...] = (query_ref[...].astype(f32) * (long_out + skipped)).astype(bf16)

    edge.wait_send()
    for place, send_ref in enumerate([send_h, send_g, mid_send_h, mid_send_g, mid_send_y, send_y]):
        sent(send_ref, place)


def shards(sizes, query_in, key_in, value_in, short_filter, tap_counts, long_filter, skip_gain):
    outer_count, inner_count = sizes
    fine_all, lane_all = fine_tables(outer_count, inner_count)
    coarse_rows = 2 * CHANNELS // outer_count
    far = pltpu.VMEM((outer_count, coarse_rows, LANES), bf16)
    mid = pltpu.VMEM((inner_count, 2 * ROWS // inner_count, LANES), bf16)
    anywhere = pl.BlockSpec(memory_space=pl.ANY)
    return pl.pallas_call(
        functools.partial(kernel, sizes),
        out_shape=jax.ShapeDtypeStruct((CHANNELS, LENGTH), bf16),
        in_specs=[anywhere] * 7
        + [pl.BlockSpec(memory_space=pltpu.SMEM), pl.BlockSpec(memory_space=pltpu.VMEM)],
        out_specs=pl.BlockSpec(memory_space=pltpu.VMEM),
        scratch_shapes=[
            pltpu.VMEM((CHANNELS, LENGTH), bf16),
            pltpu.VMEM((CHANNELS, LENGTH), bf16),
            pltpu.VMEM((CHANNELS, LENGTH), bf16),
            pltpu.VMEM((CHANNELS, LANES), f32),
            pltpu.VMEM((CHANNELS, LENGTH), f32),
            pltpu.VMEM(fine_all.shape, bf16),
            pltpu.VMEM(lane_all.shape, bf16),
            pltpu.VMEM((CHANNELS, LANES), bf16),
            pltpu.VMEM((LANES + LENGTH, CHANNELS), f32),
            pltpu.VMEM((LANES, CHANNELS), f32),
            pltpu.VMEM((2, 2 * ROWS, ROWS), bf16),
            pltpu.VMEM((2, ROWS, 2 * ROWS), bf16),
            *[far] * 6,
            *[mid] * 6,
            pltpu.SemaphoreType.DMA((7,)),
            pltpu.SemaphoreType.DMA((7,)),
            pltpu.SemaphoreType.DMA((7,)),
        ],
        compiler_params=pltpu.CompilerParams(collective_id=0, has_side_effects=True),
    )(
        query_in, key_in, value_in, short_filter, long_filter,
        jnp.asarray(fine_all), jnp.asarray(lane_all), tap_counts, skip_gain.reshape(1, CHANNELS),
    )


def solution(mesh):
    placed = (
        P("chan", ("outer", "inner")),
        P("chan", ("outer", "inner")),
        P("chan", ("outer", "inner")),
        P("chan", None),
        P(),
        P("chan", ("outer", "inner")),
        P("chan"),
    )
    sizes = (mesh.shape["outer"], mesh.shape["inner"])
    return jax.shard_map(
        functools.partial(shards, sizes),
        mesh=mesh,
        in_specs=placed,
        out_specs=P("chan", ("outer", "inner")),
        check_vma=False,
    )
```

```python
import functools
import math

import jax
import jax.numpy as jnp
import numpy as np
from jax import lax
from jax.experimental import pallas as pl
from jax.experimental.pallas import tpu as pltpu
from jax.sharding import PartitionSpec as P

GROUP_CH = 16
LANES = 128
SUB = 8
PAIR = 4
CHANNELS = 128
LENGTH = 256
MESH = pl.DeviceIdType.MESH
f32 = jnp.float32
bf16 = jnp.bfloat16


def lane_tables():
    steps = np.arange(LANES)
    angle = 2.0 * np.pi / LANES * (steps[:, None] * steps[None] % LANES)
    cos, sin = np.cos(angle), np.sin(angle)
    table = np.block([[cos, -sin], [sin, cos]])
    parts = []
    for one in (table, table.T):
        high = one.astype(bf16)
        parts += [high, (one - high.astype(np.float64)).astype(bf16)]
    return np.stack(parts)


def cos_turns(steps, period):
    half = period // 2
    centred = ((steps + half) & (period - 1)) - half
    x = centred.astype(f32) * (math.pi / period)
    y = x * x
    tail = y * (-1.0 / 5040 + y * (1.0 / 362880 - y * (1.0 / 39916800)))
    s = x * (1.0 + y * (-1.0 / 6 + y * (1.0 / 120 + tail)))
    return 1.0 - 2.0 * s * s


def split(value):
    high = value.astype(bf16)
    return high, (value - high.astype(f32)).astype(bf16)


def dot(left, right):
    return jnp.dot(left, right, preferred_element_type=f32)


def iota(shape, dim):
    return lax.broadcasted_iota(jnp.int32, shape, dim)


def turned(value, table, inverse=False):
    real, imag = value
    cos, sin = table
    if inverse:
        return real * cos - imag * sin, imag * cos + real * sin
    return real * cos + imag * sin, imag * cos - real * sin


def four(parts, inverse):
    (ar, ai), (br, bi), (cr, ci), (dr, di) = parts
    sr, si, tr, ti = ar + cr, ai + ci, ar - cr, ai - ci
    ur, ui, vr, vi = br + dr, bi + di, br - dr, bi - di
    one, three = (tr + vi, ti - vr), (tr - vi, ti + vr)
    if inverse:
        one, three = three, one
    return [(sr + ur, si + ui), one, (sr - ur, si - ui), three]


def scalar_turn(count, period):
    return math.cos(2.0 * math.pi * count / period), math.sin(2.0 * math.pi * count / period)


def stacked(parts, axis=0):
    return tuple(jnp.stack([part[which] for part in parts], axis=axis) for which in (0, 1))


def transform32(value, table, inverse):
    parts = four([tuple(x[8 * q : 8 * q + 8] for x in value) for q in range(4)], inverse)
    parts = [parts[0]] + [turned(parts[p], tuple(t[p - 1] for t in table), inverse) for p in (1, 2, 3)]
    value = stacked(parts)
    parts = four([tuple(x[:, 2 * q : 2 * q + 2] for x in value) for q in range(4)], inverse)
    sums, gaps = [], []
    for p, part in enumerate(parts):
        even, odd = tuple(x[:, 0] for x in part), tuple(x[:, 1] for x in part)
        if p == 2:
            odd = (-odd[1], odd[0]) if inverse else (odd[1], -odd[0])
        elif p:
            odd = turned(odd, scalar_turn(p, 8), inverse)
        sums.append(tuple(x + y for x, y in zip(even, odd)))
        gaps.append(tuple(x - y for x, y in zip(even, odd)))
    both = stacked(sums + gaps)
    return tuple(x.reshape((32,) + x.shape[2:]) for x in both)


def paired(first, second):
    low = iota(first.shape, first.ndim - 2) < PAIR
    first_moved = jnp.roll(first, PAIR, axis=first.ndim - 2)
    second_moved = jnp.roll(second, PAIR, axis=second.ndim - 2)
    return jnp.where(low, first, second_moved), jnp.where(low, first_moved, second)


def kernel(
    sizes, query_hbm, key_hbm, value_hbm, taps_hbm, filter_hbm, lane_hbm, counts_ref, skip_ref,
    out_ref,
    query_ref, key_ref, value_ref, taps_ref, filter_ref, lane_ref,
    edge_ref, window_ref, border_ref, kept_ref, skipped_ref, twist_ref, twiddle_ref, small_ref, spec_ref, start_ref,
    send_h, send_g, send_y, recv_h, recv_g, recv_y, mid_send, mid_recv,
    load_sem, far_send, far_recv, mid_send_sem, mid_recv_sem, edge_sem,
):
    outer_count, inner_count = sizes
    blocks = outer_count * inner_count
    total = blocks * LENGTH
    fine = 2 * inner_count
    outer_pos, inner_pos = lax.axis_index("outer"), lax.axis_index("inner")
    block_pos = outer_pos * inner_count + inner_pos

    def block_id(pos):
        return {"outer": pos // inner_count, "inner": lax.rem(pos, inner_count)}

    following = block_id(lax.rem(block_pos + 1, blocks))
    preceding = block_id(lax.rem(block_pos + blocks - 1, blocks))

    def order(count):
        return sorted(range(1, count), key=lambda offset: -min(offset, count - offset))

    loads = [
        pltpu.make_async_copy(source, target, load_sem.at[number])
        for number, (source, target) in enumerate(
            [
                (value_hbm, value_ref), (filter_hbm, filter_ref), (taps_hbm, taps_ref),
                (key_hbm, key_ref), (query_hbm, query_ref), (lane_hbm, lane_ref),
            ]
        )
    ]
    for load in loads:
        load.start()

    barrier = pltpu.get_barrier_semaphore()

    def greet(device):
        pl.semaphore_signal(barrier, inc=1, device_id=device, device_id_type=MESH)

    def greet_inner(step, carry):
        greet({"inner": lax.rem(inner_pos + step, inner_count)})
        return carry

    def greet_outer(step, carry):
        greet({"outer": lax.rem(outer_pos + step, outer_count)})
        return carry

    greet(following)
    greet(preceding)
    lax.fori_loop(1, inner_count, greet_inner, 0)
    lax.fori_loop(1, outer_count, greet_outer, 0)

    def to_sets(value):
        parts = [value[:, LANES * n : LANES * (n + 1)].reshape(outer_count // 2, SUB, LANES) for n in (0, 1)]
        both = jnp.stack(paired(*parts), axis=1)
        return both.reshape(outer_count, SUB, LANES).astype(bf16)

    def arrived(ref, sem):
        pltpu.make_async_copy(ref, ref, sem).wait()

    def sent(ref, count, sem):
        part = ref.at[pl.ds(0, count)]
        pltpu.make_async_copy(part, part, sem).wait()

    def to_outer(send_ref, recv_ref, stream):
        for offset in order(outer_count):
            target = lax.rem(outer_pos + offset, outer_count)
            pltpu.make_async_remote_copy(
                src_ref=send_ref.at[target], dst_ref=recv_ref.at[outer_pos],
                send_sem=far_send.at[stream], recv_sem=far_recv.at[stream],
                device_id={"outer": target}, device_id_type=MESH,
            ).start()
        pltpu.make_async_copy(send_ref.at[outer_pos], recv_ref.at[outer_pos], far_recv.at[stream]).start()

    loads[1].wait()
    send_h[...] = to_sets(filter_ref[...])
    loads[0].wait()
    window_ref[:LANES, :] = jnp.zeros((LANES, CHANNELS), f32)
    window_ref[LANES:, :] = jnp.transpose(value_ref[...].astype(f32))
    border_ref[LANES:, :] = jnp.zeros((LANES, CHANNELS), f32)

    pl.semaphore_wait(barrier, outer_count + inner_count)
    edge = pltpu.make_async_remote_copy(
        src_ref=value_ref.at[:, pl.ds(LANES, LANES)], dst_ref=edge_ref,
        send_sem=edge_sem.at[0], recv_sem=edge_sem.at[1],
        device_id=following, device_id_type=MESH,
    )

    edge.start()
    to_outer(send_h, recv_h, 0)

    loads[2].wait()
    lane = iota((1, LANES), 1)
    counts = jnp.zeros((1, LANES), jnp.int32)
    first_group = lax.axis_index("chan") * (CHANNELS // GROUP_CH)
    for group in range(CHANNELS // GROUP_CH):
        counts = jnp.where(lane // GROUP_CH == group, counts_ref[first_group + group], counts)
    live = iota((LANES, CHANNELS), 0) < counts
    kept_ref[...] = jnp.where(live, jnp.transpose(taps_ref[...]), 0.0)

    def short_filter(source_ref, start, rows, first):
        def eight(step, acc):
            for one in range(8):
                tap = step * 8 + one
                acc = acc + kept_ref[pl.ds(tap, 1), :] * source_ref[pl.ds(start + LANES - tap, rows), :]
            return acc

        return lax.fori_loop(first // 8, LANES // 8, eight, jnp.zeros((rows, CHANNELS), f32))

    own_late = jnp.transpose(short_filter(window_ref, LANES, LANES, 0))
    own_early = short_filter(window_ref, 0, LANES, 0)

    loads[3].wait()

    edge.wait_recv()
    before = jnp.transpose(edge_ref[...].astype(f32))
    border_ref[:LANES, :] = jnp.where(block_pos == 0, jnp.zeros_like(before), before)

    pieces = [short_filter(border_ref, 64 * n, 64, 64 * n) for n in (0, 1)]
    short_early = jnp.transpose(own_early + jnp.concatenate(pieces, axis=0))
    gated = key_ref[...].astype(f32) * jnp.concatenate([short_early, own_late], axis=1)
    send_g[...] = to_sets(gated)
    to_outer(send_g, recv_g, 1)

    skip_eye = iota((CHANNELS, CHANNELS), 0) == iota((CHANNELS, CHANNELS), 1)
    skip_col = jnp.sum(jnp.where(skip_eye, skip_ref[...], 0.0), axis=1, keepdims=True)
    skipped_ref[...] = skip_col * gated
    loads[4].wait()
    loads[5].wait()

    shape = (fine, SUB, LANES)
    lead, near = iota(shape, 0), iota(shape, 2)
    freq = 4 * (2 * inner_pos + iota(shape, 1) // PAIR) + 1
    small_shape = (24, SUB, LANES)
    small_turn = (iota(small_shape, 0) // 8 + 1) * (iota(small_shape, 0) & 7)
    for number, shift in ((0, 0), (1, 3)):
        start_ref[number] = cos_turns(lead + shift * outer_count, 4 * outer_count)
        small_ref[number] = cos_turns(small_turn + shift * 8, 32)
        twist_ref[number] = cos_turns(freq * lead + shift * outer_count * fine, 4 * outer_count * fine)
        twiddle_ref[number] = cos_turns((freq + 4 * outer_count * lead) * near + shift * total, 4 * total)

    def pair(ref):
        return ref[0], ref[1]

    def small():
        return tuple(small_ref[number].reshape(3, 8, SUB, LANES) for number in (0, 1))

    def exchange_inner(stream):
        for offset in order(inner_count):
            peer = lax.rem(inner_pos + offset, inner_count)
            pltpu.make_async_remote_copy(
                src_ref=mid_send.at[stream, peer], dst_ref=mid_recv.at[stream, inner_pos],
                send_sem=mid_send_sem.at[stream], recv_sem=mid_recv_sem.at[stream],
                device_id={"inner": peer}, device_id_type=MESH,
            ).start()
        pltpu.make_async_copy(
            mid_send.at[stream, inner_pos], mid_recv.at[stream, inner_pos], mid_recv_sem.at[stream]
        ).start()

    def mid_message(halves):
        both = jnp.stack([halves[0][0], halves[0][1], halves[1][0], halves[1][1]], axis=1)
        return both.reshape(inner_count, 4 * SUB, LANES).astype(bf16)

    def coarse_forward(recv_ref, stream):
        arrived(recv_ref, far_recv.at[stream])
        value = recv_ref[...].astype(f32)
        value = transform32((value * start_ref[0], -value * start_ref[1]), small(), False)
        parts = [x.reshape(inner_count, 2, SUB, LANES) for x in value]
        real, imag = [paired(x[:, 0], x[:, 1]) for x in parts]
        mid_send[stream] = mid_message([(real[0], imag[0]), (real[1], imag[1])])
        exchange_inner(stream)

    def fine_forward(stream):
        arrived(mid_recv.at[stream], mid_recv_sem.at[stream])
        both = mid_recv[stream].astype(f32).reshape(fine, 2, SUB, LANES)
        value = transform32(turned((both[:, 0], both[:, 1]), pair(twist_ref)), small(), False)
        value = turned(value, pair(twiddle_ref))
        block = jnp.concatenate([x.reshape(fine * SUB, LANES) for x in value], axis=1)
        high, low = split(block)
        return dot(high, lane_ref[0]) + dot(low, lane_ref[0]) + dot(high, lane_ref[1])

    def halves(spec):
        return spec[:, :LANES], spec[:, LANES:]

    coarse_forward(recv_h, 0)
    coarse_forward(recv_g, 1)
    spec_ref[...] = fine_forward(0) * (1.0 / total)
    (ar, ai), (br, bi) = halves(spec_ref[...]), halves(fine_forward(1))
    high, low = split(jnp.concatenate([ar * br - ai * bi, ar * bi + ai * br], axis=1))
    block = dot(high, lane_ref[2]) + dot(low, lane_ref[2]) + dot(high, lane_ref[3])
    value = tuple(x.reshape(fine, SUB, LANES) for x in halves(block))
    value = transform32(turned(value, pair(twiddle_ref), True), small(), True)
    value = tuple(x.reshape(inner_count, 2, SUB, LANES) for x in turned(value, pair(twist_ref), True))
    mid_send[2] = mid_message([(value[0][:, n], value[1][:, n]) for n in (0, 1)])
    exchange_inner(2)

    arrived(mid_recv.at[2], mid_recv_sem.at[2])
    both = mid_recv[2].astype(f32).reshape(inner_count, 2, 2, SUB, LANES)
    parts = [jnp.stack(paired(both[:, 0, n], both[:, 1, n]), axis=1) for n in (0, 1)]
    real, imag = transform32(tuple(x.reshape(outer_count, SUB, LANES) for x in parts), small(), True)
    send_y[...] = (real * start_ref[0] - imag * start_ref[1]).astype(bf16)
    to_outer(send_y, recv_y, 2)

    arrived(recv_y, far_recv.at[2])
    sets = recv_y[...].astype(f32).reshape(outer_count // 2, 2, SUB, LANES)
    for n, long_out in enumerate(paired(sets[:, 0], sets[:, 1])):
        span = pl.ds(LANES * n, LANES)
        long_out = long_out.reshape(CHANNELS, LANES)
        out_ref[:, span] = (query_ref[:, span].astype(f32) * (long_out + skipped_ref[:, span])).astype(bf16)

    edge.wait_send()
    for stream, send_ref in enumerate((send_h, send_g, send_y)):
        sent(send_ref, outer_count - 1, far_send.at[stream])
        sent(mid_send.at[stream], inner_count - 1, mid_send_sem.at[stream])


def shards(sizes, query_in, key_in, value_in, short_filter, tap_counts, long_filter, skip_gain):
    outer_count, inner_count = sizes
    lane_all = lane_tables()
    sets = (outer_count, SUB, LANES)
    fine = (2 * inner_count, SUB, LANES)
    anywhere = pl.BlockSpec(memory_space=pl.ANY)
    return pl.pallas_call(
        functools.partial(kernel, sizes),
        out_shape=jax.ShapeDtypeStruct((CHANNELS, LENGTH), bf16),
        in_specs=[anywhere] * 6
        + [pl.BlockSpec(memory_space=pltpu.SMEM), pl.BlockSpec(memory_space=pltpu.VMEM)],
        out_specs=pl.BlockSpec(memory_space=pltpu.VMEM),
        scratch_shapes=[
            pltpu.VMEM((CHANNELS, LENGTH), bf16),
            pltpu.VMEM((CHANNELS, LENGTH), bf16),
            pltpu.VMEM((CHANNELS, LENGTH), bf16),
            pltpu.VMEM((CHANNELS, LANES), f32),
            pltpu.VMEM((CHANNELS, LENGTH), f32),
            pltpu.VMEM(lane_all.shape, bf16),
            pltpu.VMEM((CHANNELS, LANES), bf16),
            pltpu.VMEM((LANES + LENGTH, CHANNELS), f32),
            pltpu.VMEM((2 * LANES, CHANNELS), f32),
            pltpu.VMEM((LANES, CHANNELS), f32),
            pltpu.VMEM((CHANNELS, LENGTH), f32),
            pltpu.VMEM((2, *fine), f32),
            pltpu.VMEM((2, *fine), f32),
            pltpu.VMEM((2, 24, SUB, LANES), f32),
            pltpu.VMEM((fine[0] * SUB, 2 * LANES), f32),
            pltpu.VMEM((2, *fine), f32),
            *[pltpu.VMEM(sets, bf16)] * 6,
            pltpu.VMEM((3, inner_count, 4 * SUB, LANES), bf16),
            pltpu.VMEM((3, inner_count, 4 * SUB, LANES), bf16),
            pltpu.SemaphoreType.DMA((6,)),
            pltpu.SemaphoreType.DMA((3,)),
            pltpu.SemaphoreType.DMA((3,)),
            pltpu.SemaphoreType.DMA((3,)),
            pltpu.SemaphoreType.DMA((3,)),
            pltpu.SemaphoreType.DMA((2,)),
        ],
        compiler_params=pltpu.CompilerParams(collective_id=0, has_side_effects=True),
    )(
        query_in, key_in, value_in, short_filter, long_filter,
        jnp.asarray(lane_all), tap_counts, skip_gain.reshape(1, CHANNELS),
    )


def solution(mesh):
    placed = (
        P("chan", ("outer", "inner")),
        P("chan", ("outer", "inner")),
        P("chan", ("outer", "inner")),
        P("chan", None),
        P(),
        P("chan", ("outer", "inner")),
        P("chan"),
    )
    sizes = (mesh.shape["outer"], mesh.shape["inner"])
    return jax.shard_map(
        functools.partial(shards, sizes),
        mesh=mesh,
        in_specs=placed,
        out_specs=P("chan", ("outer", "inner")),
        check_vma=False,
    )
```

```python
import functools
import math

import jax
import jax.numpy as jnp
import numpy as np
from jax import lax
from jax.experimental import pallas as pl
from jax.experimental.pallas import tpu as pltpu
from jax.sharding import PartitionSpec as P

GROUP_CH = 16
LANES = 128
SUB = 8
PAIR = 4
CHANNELS = 128
LENGTH = 256
MESH = pl.DeviceIdType.MESH
f32 = jnp.float32
bf16 = jnp.bfloat16


def lane_tables():
    steps = np.arange(LANES)
    angle = 2.0 * np.pi / LANES * (steps[:, None] * steps[None] % LANES)
    cos, sin = np.cos(angle), np.sin(angle)
    table = np.block([[cos, -sin], [sin, cos]])
    parts = []
    for one in (table, table.T):
        high = one.astype(bf16)
        parts += [high, (one - high.astype(np.float64)).astype(bf16)]
    return np.stack(parts)


def cos_turns(steps, period):
    half = period // 2
    centred = ((steps + half) & (period - 1)) - half
    x = centred.astype(f32) * (math.pi / period)
    y = x * x
    tail = y * (-1.0 / 5040 + y * (1.0 / 362880 - y * (1.0 / 39916800)))
    s = x * (1.0 + y * (-1.0 / 6 + y * (1.0 / 120 + tail)))
    return 1.0 - 2.0 * s * s


def split(value):
    high = value.astype(bf16)
    return high, (value - high.astype(f32)).astype(bf16)


def dot(left, right):
    return jnp.dot(left, right, preferred_element_type=f32)


def iota(shape, dim):
    return lax.broadcasted_iota(jnp.int32, shape, dim)


def turned(value, table, inverse=False):
    real, imag = value
    cos, sin = table
    if inverse:
        return real * cos - imag * sin, imag * cos + real * sin
    return real * cos + imag * sin, imag * cos - real * sin


def four(parts, inverse):
    (ar, ai), (br, bi), (cr, ci), (dr, di) = parts
    sr, si, tr, ti = ar + cr, ai + ci, ar - cr, ai - ci
    ur, ui, vr, vi = br + dr, bi + di, br - dr, bi - di
    one, three = (tr + vi, ti - vr), (tr - vi, ti + vr)
    if inverse:
        one, three = three, one
    return [(sr + ur, si + ui), one, (sr - ur, si - ui), three]


def scalar_turn(count, period):
    return math.cos(2.0 * math.pi * count / period), math.sin(2.0 * math.pi * count / period)


def stacked(parts, axis=0):
    return tuple(jnp.stack([part[which] for part in parts], axis=axis) for which in (0, 1))


def transform32(value, table, inverse):
    parts = four([tuple(x[8 * q : 8 * q + 8] for x in value) for q in range(4)], inverse)
    parts = [parts[0]] + [turned(parts[p], tuple(t[p - 1] for t in table), inverse) for p in (1, 2, 3)]
    value = stacked(parts)
    parts = four([tuple(x[:, 2 * q : 2 * q + 2] for x in value) for q in range(4)], inverse)
    sums, gaps = [], []
    for p, part in enumerate(parts):
        even, odd = tuple(x[:, 0] for x in part), tuple(x[:, 1] for x in part)
        if p == 2:
            odd = (-odd[1], odd[0]) if inverse else (odd[1], -odd[0])
        elif p:
            odd = turned(odd, scalar_turn(p, 8), inverse)
        sums.append(tuple(x + y for x, y in zip(even, odd)))
        gaps.append(tuple(x - y for x, y in zip(even, odd)))
    both = stacked(sums + gaps)
    return tuple(x.reshape((32,) + x.shape[2:]) for x in both)


def paired(first, second):
    low = iota(first.shape, first.ndim - 2) < PAIR
    first_moved = jnp.roll(first, PAIR, axis=first.ndim - 2)
    second_moved = jnp.roll(second, PAIR, axis=second.ndim - 2)
    return jnp.where(low, first, second_moved), jnp.where(low, first_moved, second)


def kernel(
    sizes, query_hbm, key_hbm, value_hbm, taps_hbm, filter_hbm, lane_hbm, counts_ref, skip_ref,
    out_ref,
    query_ref, key_ref, value_ref, taps_ref, filter_ref, lane_ref,
    edge_ref, window_ref, kept_ref, skipped_ref, twist_ref, twiddle_ref, small_ref, spec_ref, start_ref,
    send_h, send_g, send_y, recv_h, recv_g, recv_y, mid_send, mid_recv,
    load_sem, far_send, far_recv, mid_send_sem, mid_recv_sem, edge_sem,
):
    outer_count, inner_count = sizes
    blocks = outer_count * inner_count
    total = blocks * LENGTH
    fine = 2 * inner_count
    outer_pos, inner_pos = lax.axis_index("outer"), lax.axis_index("inner")
    block_pos = outer_pos * inner_count + inner_pos

    def block_id(pos):
        return {"outer": pos // inner_count, "inner": lax.rem(pos, inner_count)}

    following = block_id(lax.rem(block_pos + 1, blocks))
    preceding = block_id(lax.rem(block_pos + blocks - 1, blocks))

    def order(count):
        return sorted(range(1, count), key=lambda offset: -min(offset, count - offset))

    loads = [
        pltpu.make_async_copy(source, target, load_sem.at[number])
        for number, (source, target) in enumerate(
            [
                (value_hbm, value_ref), (filter_hbm, filter_ref), (taps_hbm, taps_ref),
                (key_hbm, key_ref), (query_hbm, query_ref), (lane_hbm, lane_ref),
            ]
        )
    ]
    for load in loads:
        load.start()

    barrier = pltpu.get_barrier_semaphore()

    def greet(device):
        pl.semaphore_signal(barrier, inc=1, device_id=device, device_id_type=MESH)

    for offset in order(outer_count):
        greet({"outer": lax.rem(outer_pos + offset, outer_count)})
    for offset in order(inner_count):
        greet({"inner": lax.rem(inner_pos + offset, inner_count)})
    greet(following)
    greet(preceding)

    def to_sets(value):
        parts = [value[:, LANES * n : LANES * (n + 1)].reshape(outer_count // 2, SUB, LANES) for n in (0, 1)]
        both = jnp.stack(paired(*parts), axis=1)
        return both.reshape(outer_count, SUB, LANES).astype(bf16)

    def arrived(ref, sem):
        pltpu.make_async_copy(ref, ref, sem).wait()

    def sent(ref, count, sem):
        part = ref.at[pl.ds(0, count)]
        pltpu.make_async_copy(part, part, sem).wait()

    def to_outer(send_ref, recv_ref, stream):
        for offset in order(outer_count):
            target = lax.rem(outer_pos + offset, outer_count)
            pltpu.make_async_remote_copy(
                src_ref=send_ref.at[target], dst_ref=recv_ref.at[outer_pos],
                send_sem=far_send.at[stream], recv_sem=far_recv.at[stream],
                device_id={"outer": target}, device_id_type=MESH,
            ).start()
        pltpu.make_async_copy(send_ref.at[outer_pos], recv_ref.at[outer_pos], far_recv.at[stream]).start()

    loads[1].wait()
    send_h[...] = to_sets(filter_ref[...])
    loads[0].wait()
    window_ref[LANES:, :] = jnp.transpose(value_ref[...].astype(f32))

    pl.semaphore_wait(barrier, outer_count + inner_count)
    edge = pltpu.make_async_remote_copy(
        src_ref=value_ref.at[:, pl.ds(LANES, LANES)], dst_ref=edge_ref,
        send_sem=edge_sem.at[0], recv_sem=edge_sem.at[1],
        device_id=following, device_id_type=MESH,
    )

    edge.start()
    to_outer(send_h, recv_h, 0)

    loads[2].wait()
    lane = iota((1, LANES), 1)
    counts = jnp.zeros((1, LANES), jnp.int32)
    first_group = lax.axis_index("chan") * (CHANNELS // GROUP_CH)
    for group in range(CHANNELS // GROUP_CH):
        counts = jnp.where(lane // GROUP_CH == group, counts_ref[first_group + group], counts)
    live = iota((LANES, CHANNELS), 0) < counts
    kept_ref[...] = jnp.where(live, jnp.transpose(taps_ref[...]), 0.0)

    groups = LANES // SUB

    def tap(residue, step):
        return kept_ref[pl.ds(residue + SUB * step, 1), :]

    def short_late(residue, acc):
        rows = SUB * (2 * groups - 1)
        block = window_ref[pl.ds(LANES + SUB - residue, rows), :]
        for step in range(groups):
            start = SUB * (groups - 1 - step)
            acc = acc + tap(residue, step) * block[start : start + LANES]
        return acc

    def short_early(first, pairs):
        def one(residue, acc):
            acc = list(acc)
            block = window_ref[pl.ds(first - residue, LANES), :]
            for step in range(groups):
                weight = tap(residue, step)
                for place, source in pairs(step):
                    acc[place] = acc[place] + weight * block[SUB * source : SUB * (source + 1)]
            return tuple(acc)

        return one

    def own_pairs(step):
        return [(place, place - step - 1) for place in range(step + 1, groups)]

    def edge_pairs(step):
        return [(place, groups - 1 + place - step) for place in range(step + 1)]

    own_late = jnp.transpose(lax.fori_loop(0, SUB, short_late, jnp.zeros((LANES, CHANNELS), f32)))
    early = tuple(jnp.zeros((SUB, CHANNELS), f32) for _ in range(groups))
    early = lax.fori_loop(0, SUB, short_early(LANES + SUB, own_pairs), early)

    loads[3].wait()

    edge.wait_recv()
    before = jnp.transpose(edge_ref[...].astype(f32))
    window_ref[:LANES, :] = jnp.where(block_pos == 0, jnp.zeros_like(before), before)

    early = lax.fori_loop(0, SUB, short_early(SUB, edge_pairs), early)
    short_out = jnp.transpose(jnp.concatenate(early, axis=0))
    gated = key_ref[...].astype(f32) * jnp.concatenate([short_out, own_late], axis=1)
    send_g[...] = to_sets(gated)
    to_outer(send_g, recv_g, 1)

    skip_eye = iota((CHANNELS, CHANNELS), 0) == iota((CHANNELS, CHANNELS), 1)
    skip_col = jnp.sum(jnp.where(skip_eye, skip_ref[...], 0.0), axis=1, keepdims=True)
    skipped_ref[...] = skip_col * gated
    loads[4].wait()
    loads[5].wait()

    shape = (fine, SUB, LANES)
    lead, near = iota(shape, 0), iota(shape, 2)
    freq = 4 * (2 * inner_pos + iota(shape, 1) // PAIR) + 1
    small_shape = (24, SUB, LANES)
    small_turn = (iota(small_shape, 0) // 8 + 1) * (iota(small_shape, 0) & 7)
    for number, shift in ((0, 0), (1, 3)):
        start_ref[number] = cos_turns(lead + shift * outer_count, 4 * outer_count)
        small_ref[number] = cos_turns(small_turn + shift * 8, 32)
        twist_ref[number] = cos_turns(freq * lead + shift * outer_count * fine, 4 * outer_count * fine)
        twiddle_ref[number] = cos_turns((freq + 4 * outer_count * lead) * near + shift * total, 4 * total)

    def pair(ref):
        return ref[0], ref[1]

    def small():
        return tuple(small_ref[number].reshape(3, 8, SUB, LANES) for number in (0, 1))

    def exchange_inner(stream):
        for offset in order(inner_count):
            peer = lax.rem(inner_pos + offset, inner_count)
            pltpu.make_async_remote_copy(
                src_ref=mid_send.at[stream, peer], dst_ref=mid_recv.at[stream, inner_pos],
                send_sem=mid_send_sem.at[stream], recv_sem=mid_recv_sem.at[stream],
                device_id={"inner": peer}, device_id_type=MESH,
            ).start()
        pltpu.make_async_copy(
            mid_send.at[stream, inner_pos], mid_recv.at[stream, inner_pos], mid_recv_sem.at[stream]
        ).start()

    def mid_message(halves):
        both = jnp.stack([halves[0][0], halves[0][1], halves[1][0], halves[1][1]], axis=1)
        return both.reshape(inner_count, 4 * SUB, LANES).astype(bf16)

    def coarse_forward(recv_ref, stream):
        arrived(recv_ref, far_recv.at[stream])
        value = recv_ref[...].astype(f32)
        value = transform32((value * start_ref[0], -value * start_ref[1]), small(), False)
        parts = [x.reshape(inner_count, 2, SUB, LANES) for x in value]
        real, imag = [paired(x[:, 0], x[:, 1]) for x in parts]
        mid_send[stream] = mid_message([(real[0], imag[0]), (real[1], imag[1])])
        exchange_inner(stream)

    def fine_forward(stream):
        arrived(mid_recv.at[stream], mid_recv_sem.at[stream])
        both = mid_recv[stream].astype(f32).reshape(fine, 2, SUB, LANES)
        value = transform32(turned((both[:, 0], both[:, 1]), pair(twist_ref)), small(), False)
        value = turned(value, pair(twiddle_ref))
        block = jnp.concatenate([x.reshape(fine * SUB, LANES) for x in value], axis=1)
        high, low = split(block)
        return dot(high, lane_ref[0]) + dot(low, lane_ref[0]) + dot(high, lane_ref[1])

    def halves(spec):
        return spec[:, :LANES], spec[:, LANES:]

    coarse_forward(recv_h, 0)
    coarse_forward(recv_g, 1)
    spec_ref[...] = fine_forward(0) * (1.0 / total)
    (ar, ai), (br, bi) = halves(spec_ref[...]), halves(fine_forward(1))
    high, low = split(jnp.concatenate([ar * br - ai * bi, ar * bi + ai * br], axis=1))
    block = dot(high, lane_ref[2]) + dot(low, lane_ref[2]) + dot(high, lane_ref[3])
    value = tuple(x.reshape(fine, SUB, LANES) for x in halves(block))
    value = transform32(turned(value, pair(twiddle_ref), True), small(), True)
    value = tuple(x.reshape(inner_count, 2, SUB, LANES) for x in turned(value, pair(twist_ref), True))
    mid_send[2] = mid_message([(value[0][:, n], value[1][:, n]) for n in (0, 1)])
    exchange_inner(2)

    arrived(mid_recv.at[2], mid_recv_sem.at[2])
    both = mid_recv[2].astype(f32).reshape(inner_count, 2, 2, SUB, LANES)
    parts = [jnp.stack(paired(both[:, 0, n], both[:, 1, n]), axis=1) for n in (0, 1)]
    real, imag = transform32(tuple(x.reshape(outer_count, SUB, LANES) for x in parts), small(), True)
    send_y[...] = (real * start_ref[0] - imag * start_ref[1]).astype(bf16)
    to_outer(send_y, recv_y, 2)

    arrived(recv_y, far_recv.at[2])
    sets = recv_y[...].astype(f32).reshape(outer_count // 2, 2, SUB, LANES)
    for n, long_out in enumerate(paired(sets[:, 0], sets[:, 1])):
        span = pl.ds(LANES * n, LANES)
        long_out = long_out.reshape(CHANNELS, LANES)
        out_ref[:, span] = (query_ref[:, span].astype(f32) * (long_out + skipped_ref[:, span])).astype(bf16)

    edge.wait_send()
    for stream, send_ref in enumerate((send_h, send_g, send_y)):
        sent(send_ref, outer_count - 1, far_send.at[stream])
        sent(mid_send.at[stream], inner_count - 1, mid_send_sem.at[stream])


def shards(sizes, query_in, key_in, value_in, short_filter, tap_counts, long_filter, skip_gain):
    outer_count, inner_count = sizes
    lane_all = lane_tables()
    sets = (outer_count, SUB, LANES)
    fine = (2 * inner_count, SUB, LANES)
    anywhere = pl.BlockSpec(memory_space=pl.ANY)
    return pl.pallas_call(
        functools.partial(kernel, sizes),
        out_shape=pltpu.VMEM((CHANNELS, LENGTH), bf16),
        in_specs=[anywhere] * 6
        + [pl.BlockSpec(memory_space=pltpu.SMEM), pl.BlockSpec(memory_space=pltpu.VMEM)],
        out_specs=pl.BlockSpec(memory_space=pltpu.VMEM),
        scratch_shapes=[
            pltpu.VMEM((CHANNELS, LENGTH), bf16),
            pltpu.VMEM((CHANNELS, LENGTH), bf16),
            pltpu.VMEM((CHANNELS, LENGTH), bf16),
            pltpu.VMEM((CHANNELS, LANES), f32),
            pltpu.VMEM((CHANNELS, LENGTH), f32),
            pltpu.VMEM(lane_all.shape, bf16),
            pltpu.VMEM((CHANNELS, LANES), bf16),
            pltpu.VMEM((LANES + LENGTH, CHANNELS), f32),
            pltpu.VMEM((LANES, CHANNELS), f32),
            pltpu.VMEM((CHANNELS, LENGTH), f32),
            pltpu.VMEM((2, *fine), f32),
            pltpu.VMEM((2, *fine), f32),
            pltpu.VMEM((2, 24, SUB, LANES), f32),
            pltpu.VMEM((fine[0] * SUB, 2 * LANES), f32),
            pltpu.VMEM((2, *fine), f32),
            *[pltpu.VMEM(sets, bf16)] * 6,
            pltpu.VMEM((3, inner_count, 4 * SUB, LANES), bf16),
            pltpu.VMEM((3, inner_count, 4 * SUB, LANES), bf16),
            pltpu.SemaphoreType.DMA((6,)),
            pltpu.SemaphoreType.DMA((3,)),
            pltpu.SemaphoreType.DMA((3,)),
            pltpu.SemaphoreType.DMA((3,)),
            pltpu.SemaphoreType.DMA((3,)),
            pltpu.SemaphoreType.DMA((2,)),
        ],
        compiler_params=pltpu.CompilerParams(collective_id=0, has_side_effects=True),
    )(
        query_in, key_in, value_in, short_filter, long_filter,
        jnp.asarray(lane_all), tap_counts, skip_gain.reshape(1, CHANNELS),
    )


def solution(mesh):
    placed = (
        P("chan", ("outer", "inner")),
        P("chan", ("outer", "inner")),
        P("chan", ("outer", "inner")),
        P("chan", None),
        P(),
        P("chan", ("outer", "inner")),
        P("chan"),
    )
    sizes = (mesh.shape["outer"], mesh.shape["inner"])
    return jax.shard_map(
        functools.partial(shards, sizes),
        mesh=mesh,
        in_specs=placed,
        out_specs=P("chan", ("outer", "inner")),
        check_vma=False,
    )
```

```python
import functools
import math

import jax
import jax.numpy as jnp
import numpy as np
from jax import lax
from jax.experimental import pallas as pl
from jax.experimental.pallas import tpu as pltpu
from jax.sharding import PartitionSpec as P

GROUP_CH = 16
LANES = 128
SUB = 8
PAIR = 4
CHANNELS = 128
LENGTH = 256
MESH = pl.DeviceIdType.MESH
f32 = jnp.float32
bf16 = jnp.bfloat16


def lane_tables():
    steps = np.arange(LANES)
    angle = 2.0 * np.pi / LANES * (steps[:, None] * steps[None] % LANES)
    cos, sin = np.cos(angle), np.sin(angle)
    table = np.block([[cos, -sin], [sin, cos]])
    parts = []
    for one in (table, table.T):
        high = one.astype(bf16)
        parts += [high, (one - high.astype(np.float64)).astype(bf16)]
    return np.stack(parts)


def cos_turns(steps, period):
    half = period // 2
    centred = ((steps + half) & (period - 1)) - half
    x = centred.astype(f32) * (math.pi / period)
    y = x * x
    tail = y * (-1.0 / 5040 + y * (1.0 / 362880 - y * (1.0 / 39916800)))
    s = x * (1.0 + y * (-1.0 / 6 + y * (1.0 / 120 + tail)))
    return 1.0 - 2.0 * s * s


def split(value):
    high = value.astype(bf16)
    return high, (value - high.astype(f32)).astype(bf16)


def dot(left, right):
    return jnp.dot(left, right, preferred_element_type=f32)


def iota(shape, dim):
    return lax.broadcasted_iota(jnp.int32, shape, dim)


def turned(value, table, inverse=False):
    real, imag = value
    cos, sin = table
    if inverse:
        return real * cos - imag * sin, imag * cos + real * sin
    return real * cos + imag * sin, imag * cos - real * sin


def four(parts, inverse):
    (ar, ai), (br, bi), (cr, ci), (dr, di) = parts
    sr, si, tr, ti = ar + cr, ai + ci, ar - cr, ai - ci
    ur, ui, vr, vi = br + dr, bi + di, br - dr, bi - di
    one, three = (tr + vi, ti - vr), (tr - vi, ti + vr)
    if inverse:
        one, three = three, one
    return [(sr + ur, si + ui), one, (sr - ur, si - ui), three]


def scalar_turn(count, period):
    return math.cos(2.0 * math.pi * count / period), math.sin(2.0 * math.pi * count / period)


def stacked(parts, axis=0):
    return tuple(jnp.stack([part[which] for part in parts], axis=axis) for which in (0, 1))


def transform32(value, table, inverse):
    parts = four([tuple(x[8 * q : 8 * q + 8] for x in value) for q in range(4)], inverse)
    parts = [parts[0]] + [turned(parts[p], tuple(t[p - 1] for t in table), inverse) for p in (1, 2, 3)]
    value = stacked(parts)
    parts = four([tuple(x[:, 2 * q : 2 * q + 2] for x in value) for q in range(4)], inverse)
    sums, gaps = [], []
    for p, part in enumerate(parts):
        even, odd = tuple(x[:, 0] for x in part), tuple(x[:, 1] for x in part)
        if p == 2:
            odd = (-odd[1], odd[0]) if inverse else (odd[1], -odd[0])
        elif p:
            odd = turned(odd, scalar_turn(p, 8), inverse)
        sums.append(tuple(x + y for x, y in zip(even, odd)))
        gaps.append(tuple(x - y for x, y in zip(even, odd)))
    both = stacked(sums + gaps)
    return tuple(x.reshape((32,) + x.shape[2:]) for x in both)


def paired(first, second):
    low = iota(first.shape, first.ndim - 2) < PAIR
    first_moved = jnp.roll(first, PAIR, axis=first.ndim - 2)
    second_moved = jnp.roll(second, PAIR, axis=second.ndim - 2)
    return jnp.where(low, first, second_moved), jnp.where(low, first_moved, second)


def kernel(
    sizes, query_hbm, key_hbm, value_hbm, taps_hbm, filter_hbm, lane_hbm, counts_hbm, skip_hbm,
    out_ref,
    query_ref, key_ref, value_ref, taps_ref, filter_ref, lane_ref, counts_ref, skip_ref,
    edge_ref, window_ref, kept_ref, skipped_ref, twist_ref, twiddle_ref, small_ref, spec_ref, start_ref,
    send_h, send_g, send_y, recv_h, recv_g, recv_y, mid_send, mid_recv,
    load_sem, far_send, far_recv, mid_send_sem, mid_recv_sem, edge_sem,
):
    outer_count, inner_count = sizes
    blocks = outer_count * inner_count
    total = blocks * LENGTH
    fine = 2 * inner_count
    outer_pos, inner_pos = lax.axis_index("outer"), lax.axis_index("inner")
    block_pos = outer_pos * inner_count + inner_pos

    def block_id(pos):
        return {"outer": pos // inner_count, "inner": lax.rem(pos, inner_count)}

    following = block_id(lax.rem(block_pos + 1, blocks))
    preceding = block_id(lax.rem(block_pos + blocks - 1, blocks))

    def order(count):
        return sorted(range(1, count), key=lambda offset: -min(offset, count - offset))

    loads = [
        pltpu.make_async_copy(source, target, load_sem.at[number])
        for number, (source, target) in enumerate(
            [
                (value_hbm, value_ref), (filter_hbm, filter_ref), (taps_hbm, taps_ref),
                (key_hbm, key_ref), (query_hbm, query_ref), (lane_hbm, lane_ref),
                (counts_hbm, counts_ref), (skip_hbm, skip_ref),
            ]
        )
    ]
    for load in loads:
        load.start()

    barrier = pltpu.get_barrier_semaphore()

    def greet(device):
        pl.semaphore_signal(barrier, inc=1, device_id=device, device_id_type=MESH)

    for offset in order(outer_count):
        greet({"outer": lax.rem(outer_pos + offset, outer_count)})
    for offset in order(inner_count):
        greet({"inner": lax.rem(inner_pos + offset, inner_count)})
    greet(following)
    greet(preceding)

    def to_sets(value):
        parts = [value[:, LANES * n : LANES * (n + 1)].reshape(outer_count // 2, SUB, LANES) for n in (0, 1)]
        both = jnp.stack(paired(*parts), axis=1)
        return both.reshape(outer_count, SUB, LANES).astype(bf16)

    def arrived(ref, sem):
        pltpu.make_async_copy(ref, ref, sem).wait()

    def sent(ref, count, sem):
        part = ref.at[pl.ds(0, count)]
        pltpu.make_async_copy(part, part, sem).wait()

    def to_outer(send_ref, recv_ref, stream):
        for offset in order(outer_count):
            target = lax.rem(outer_pos + offset, outer_count)
            pltpu.make_async_remote_copy(
                src_ref=send_ref.at[target], dst_ref=recv_ref.at[outer_pos],
                send_sem=far_send.at[stream], recv_sem=far_recv.at[stream],
                device_id={"outer": target}, device_id_type=MESH,
            ).start()
        pltpu.make_async_copy(send_ref.at[outer_pos], recv_ref.at[outer_pos], far_recv.at[stream]).start()

    loads[1].wait()
    send_h[...] = to_sets(filter_ref[...])
    loads[0].wait()
    window_ref[LANES:, :] = jnp.transpose(value_ref[...].astype(f32))

    pl.semaphore_wait(barrier, outer_count + inner_count)
    edge = pltpu.make_async_remote_copy(
        src_ref=value_ref.at[:, pl.ds(LANES, LANES)], dst_ref=edge_ref,
        send_sem=edge_sem.at[0], recv_sem=edge_sem.at[1],
        device_id=following, device_id_type=MESH,
    )

    edge.start()
    to_outer(send_h, recv_h, 0)

    loads[2].wait()
    loads[6].wait()
    lane = iota((1, LANES), 1)
    counts = jnp.zeros((1, LANES), jnp.int32)
    first_group = lax.axis_index("chan") * (CHANNELS // GROUP_CH)
    for group in range(CHANNELS // GROUP_CH):
        counts = jnp.where(lane // GROUP_CH == group, counts_ref[first_group + group], counts)
    live = iota((LANES, CHANNELS), 0) < counts
    kept_ref[...] = jnp.where(live, jnp.transpose(taps_ref[...]), 0.0)

    groups = LANES // SUB

    def tap(residue, step):
        return kept_ref[pl.ds(residue + SUB * step, 1), :]

    def short_late(residue, acc):
        rows = SUB * (2 * groups - 1)
        block = window_ref[pl.ds(LANES + SUB - residue, rows), :]
        for step in range(groups):
            start = SUB * (groups - 1 - step)
            acc = acc + tap(residue, step) * block[start : start + LANES]
        return acc

    def short_early(first, pairs):
        def one(residue, acc):
            acc = list(acc)
            block = window_ref[pl.ds(first - residue, LANES), :]
            for step in range(groups):
                weight = tap(residue, step)
                for place, source in pairs(step):
                    acc[place] = acc[place] + weight * block[SUB * source : SUB * (source + 1)]
            return tuple(acc)

        return one

    def own_pairs(step):
        return [(place, place - step - 1) for place in range(step + 1, groups)]

    def edge_pairs(step):
        return [(place, groups - 1 + place - step) for place in range(step + 1)]

    own_late = jnp.transpose(lax.fori_loop(0, SUB, short_late, jnp.zeros((LANES, CHANNELS), f32)))
    early = tuple(jnp.zeros((SUB, CHANNELS), f32) for _ in range(groups))
    early = lax.fori_loop(0, SUB, short_early(LANES + SUB, own_pairs), early)

    loads[3].wait()

    edge.wait_recv()
    before = jnp.transpose(edge_ref[...].astype(f32))
    window_ref[:LANES, :] = jnp.where(block_pos == 0, jnp.zeros_like(before), before)

    early = lax.fori_loop(0, SUB, short_early(SUB, edge_pairs), early)
    short_out = jnp.transpose(jnp.concatenate(early, axis=0))
    gated = key_ref[...].astype(f32) * jnp.concatenate([short_out, own_late], axis=1)
    send_g[...] = to_sets(gated)
    to_outer(send_g, recv_g, 1)

    loads[7].wait()
    skip_eye = iota((CHANNELS, CHANNELS), 0) == iota((CHANNELS, CHANNELS), 1)
    skip_col = jnp.sum(jnp.where(skip_eye, skip_ref[...], 0.0), axis=1, keepdims=True)
    skipped_ref[...] = skip_col * gated
    loads[4].wait()
    loads[5].wait()

    shape = (fine, SUB, LANES)
    lead, near = iota(shape, 0), iota(shape, 2)
    freq = 4 * (2 * inner_pos + iota(shape, 1) // PAIR) + 1
    small_shape = (24, SUB, LANES)
    small_turn = (iota(small_shape, 0) // 8 + 1) * (iota(small_shape, 0) & 7)
    for number, shift in ((0, 0), (1, 3)):
        start_ref[number] = cos_turns(lead + shift * outer_count, 4 * outer_count)
        small_ref[number] = cos_turns(small_turn + shift * 8, 32)
        twist_ref[number] = cos_turns(freq * lead + shift * outer_count * fine, 4 * outer_count * fine)
        twiddle_ref[number] = cos_turns((freq + 4 * outer_count * lead) * near + shift * total, 4 * total)

    def pair(ref):
        return ref[0], ref[1]

    def small():
        return tuple(small_ref[number].reshape(3, 8, SUB, LANES) for number in (0, 1))

    def exchange_inner(stream):
        for offset in order(inner_count):
            peer = lax.rem(inner_pos + offset, inner_count)
            pltpu.make_async_remote_copy(
                src_ref=mid_send.at[stream, peer], dst_ref=mid_recv.at[stream, inner_pos],
                send_sem=mid_send_sem.at[stream], recv_sem=mid_recv_sem.at[stream],
                device_id={"inner": peer}, device_id_type=MESH,
            ).start()
        pltpu.make_async_copy(
            mid_send.at[stream, inner_pos], mid_recv.at[stream, inner_pos], mid_recv_sem.at[stream]
        ).start()

    def mid_message(halves):
        both = jnp.stack([halves[0][0], halves[0][1], halves[1][0], halves[1][1]], axis=1)
        return both.reshape(inner_count, 4 * SUB, LANES).astype(bf16)

    def coarse_forward(recv_ref, stream):
        arrived(recv_ref, far_recv.at[stream])
        value = recv_ref[...].astype(f32)
        value = transform32((value * start_ref[0], -value * start_ref[1]), small(), False)
        parts = [x.reshape(inner_count, 2, SUB, LANES) for x in value]
        real, imag = [paired(x[:, 0], x[:, 1]) for x in parts]
        mid_send[stream] = mid_message([(real[0], imag[0]), (real[1], imag[1])])
        exchange_inner(stream)

    def fine_forward(stream):
        arrived(mid_recv.at[stream], mid_recv_sem.at[stream])
        both = mid_recv[stream].astype(f32).reshape(fine, 2, SUB, LANES)
        value = transform32(turned((both[:, 0], both[:, 1]), pair(twist_ref)), small(), False)
        value = turned(value, pair(twiddle_ref))
        block = jnp.concatenate([x.reshape(fine * SUB, LANES) for x in value], axis=1)
        high, low = split(block)
        return dot(high, lane_ref[0]) + dot(low, lane_ref[0]) + dot(high, lane_ref[1])

    def halves(spec):
        return spec[:, :LANES], spec[:, LANES:]

    coarse_forward(recv_h, 0)
    coarse_forward(recv_g, 1)
    spec_ref[...] = fine_forward(0) * (1.0 / total)
    (ar, ai), (br, bi) = halves(spec_ref[...]), halves(fine_forward(1))
    high, low = split(jnp.concatenate([ar * br - ai * bi, ar * bi + ai * br], axis=1))
    block = dot(high, lane_ref[2]) + dot(low, lane_ref[2]) + dot(high, lane_ref[3])
    value = tuple(x.reshape(fine, SUB, LANES) for x in halves(block))
    value = transform32(turned(value, pair(twiddle_ref), True), small(), True)
    value = tuple(x.reshape(inner_count, 2, SUB, LANES) for x in turned(value, pair(twist_ref), True))
    mid_send[2] = mid_message([(value[0][:, n], value[1][:, n]) for n in (0, 1)])
    exchange_inner(2)

    arrived(mid_recv.at[2], mid_recv_sem.at[2])
    both = mid_recv[2].astype(f32).reshape(inner_count, 2, 2, SUB, LANES)
    parts = [jnp.stack(paired(both[:, 0, n], both[:, 1, n]), axis=1) for n in (0, 1)]
    real, imag = transform32(tuple(x.reshape(outer_count, SUB, LANES) for x in parts), small(), True)
    send_y[...] = (real * start_ref[0] - imag * start_ref[1]).astype(bf16)
    to_outer(send_y, recv_y, 2)

    arrived(recv_y, far_recv.at[2])
    sets = recv_y[...].astype(f32).reshape(outer_count // 2, 2, SUB, LANES)
    for n, long_out in enumerate(paired(sets[:, 0], sets[:, 1])):
        span = pl.ds(LANES * n, LANES)
        long_out = long_out.reshape(CHANNELS, LANES)
        out_ref[:, span] = (query_ref[:, span].astype(f32) * (long_out + skipped_ref[:, span])).astype(bf16)

    edge.wait_send()
    for stream, send_ref in enumerate((send_h, send_g, send_y)):
        sent(send_ref, outer_count - 1, far_send.at[stream])
        sent(mid_send.at[stream], inner_count - 1, mid_send_sem.at[stream])


def shards(sizes, query_in, key_in, value_in, short_filter, tap_counts, long_filter, skip_gain):
    outer_count, inner_count = sizes
    lane_all = lane_tables()
    sets = (outer_count, SUB, LANES)
    fine = (2 * inner_count, SUB, LANES)
    anywhere = pl.BlockSpec(memory_space=pl.ANY)
    return pl.pallas_call(
        functools.partial(kernel, sizes),
        out_shape=pltpu.VMEM((CHANNELS, LENGTH), bf16),
        in_specs=[anywhere] * 8,
        out_specs=pl.BlockSpec(memory_space=pltpu.VMEM),
        scratch_shapes=[
            pltpu.VMEM((CHANNELS, LENGTH), bf16),
            pltpu.VMEM((CHANNELS, LENGTH), bf16),
            pltpu.VMEM((CHANNELS, LENGTH), bf16),
            pltpu.VMEM((CHANNELS, LANES), f32),
            pltpu.VMEM((CHANNELS, LENGTH), f32),
            pltpu.VMEM(lane_all.shape, bf16),
            pltpu.SMEM(tap_counts.shape, jnp.int32),
            pltpu.VMEM((1, CHANNELS), f32),
            pltpu.VMEM((CHANNELS, LANES), bf16),
            pltpu.VMEM((LANES + LENGTH, CHANNELS), f32),
            pltpu.VMEM((LANES, CHANNELS), f32),
            pltpu.VMEM((CHANNELS, LENGTH), f32),
            pltpu.VMEM((2, *fine), f32),
            pltpu.VMEM((2, *fine), f32),
            pltpu.VMEM((2, 24, SUB, LANES), f32),
            pltpu.VMEM((fine[0] * SUB, 2 * LANES), f32),
            pltpu.VMEM((2, *fine), f32),
            *[pltpu.VMEM(sets, bf16)] * 6,
            pltpu.VMEM((3, inner_count, 4 * SUB, LANES), bf16),
            pltpu.VMEM((3, inner_count, 4 * SUB, LANES), bf16),
            pltpu.SemaphoreType.DMA((8,)),
            pltpu.SemaphoreType.DMA((3,)),
            pltpu.SemaphoreType.DMA((3,)),
            pltpu.SemaphoreType.DMA((3,)),
            pltpu.SemaphoreType.DMA((3,)),
            pltpu.SemaphoreType.DMA((2,)),
        ],
        compiler_params=pltpu.CompilerParams(collective_id=0, has_side_effects=True),
    )(
        query_in, key_in, value_in, short_filter, long_filter,
        jnp.asarray(lane_all), tap_counts, skip_gain.reshape(1, CHANNELS),
    )


def solution(mesh):
    placed = (
        P("chan", ("outer", "inner")),
        P("chan", ("outer", "inner")),
        P("chan", ("outer", "inner")),
        P("chan", None),
        P(),
        P("chan", ("outer", "inner")),
        P("chan"),
    )
    sizes = (mesh.shape["outer"], mesh.shape["inner"])
    return jax.shard_map(
        functools.partial(shards, sizes),
        mesh=mesh,
        in_specs=placed,
        out_specs=P("chan", ("outer", "inner")),
        check_vma=False,
    )
```

```python
import functools
import math

import jax
import jax.numpy as jnp
import numpy as np
from jax import lax
from jax.experimental import pallas as pl
from jax.experimental.pallas import tpu as pltpu
from jax.sharding import PartitionSpec as P

GROUP_CH = 16
LANES = 128
SUB = 8
PAIR = 4
CHANNELS = 128
LENGTH = 256
MESH = pl.DeviceIdType.MESH
f32 = jnp.float32
bf16 = jnp.bfloat16


def lane_tables():
    steps = np.arange(LANES)
    angle = 2.0 * np.pi / LANES * (steps[:, None] * steps[None] % LANES)
    cos, sin = np.cos(angle), np.sin(angle)
    table = np.block([[cos, -sin], [sin, cos]])
    parts = []
    for one in (table, table.T):
        high = one.astype(bf16)
        parts += [high, (one - high.astype(np.float64)).astype(bf16)]
    return np.stack(parts)


def cos_turns(steps, period):
    half = period // 2
    centred = ((steps + half) & (period - 1)) - half
    x = centred.astype(f32) * (math.pi / period)
    y = x * x
    tail = y * (-1.0 / 5040 + y * (1.0 / 362880 - y * (1.0 / 39916800)))
    s = x * (1.0 + y * (-1.0 / 6 + y * (1.0 / 120 + tail)))
    return 1.0 - 2.0 * s * s


def split(value):
    high = value.astype(bf16)
    return high, (value - high.astype(f32)).astype(bf16)


def dot(left, right):
    return jnp.dot(left, right, preferred_element_type=f32)


def iota(shape, dim):
    return lax.broadcasted_iota(jnp.int32, shape, dim)


def turned(value, table, inverse=False):
    real, imag = value
    cos, sin = table
    if inverse:
        return real * cos - imag * sin, imag * cos + real * sin
    return real * cos + imag * sin, imag * cos - real * sin


def four(parts, inverse):
    (ar, ai), (br, bi), (cr, ci), (dr, di) = parts
    sr, si, tr, ti = ar + cr, ai + ci, ar - cr, ai - ci
    ur, ui, vr, vi = br + dr, bi + di, br - dr, bi - di
    one, three = (tr + vi, ti - vr), (tr - vi, ti + vr)
    if inverse:
        one, three = three, one
    return [(sr + ur, si + ui), one, (sr - ur, si - ui), three]


def scalar_turn(count, period):
    return math.cos(2.0 * math.pi * count / period), math.sin(2.0 * math.pi * count / period)


def stacked(parts, axis=0):
    return tuple(jnp.stack([part[which] for part in parts], axis=axis) for which in (0, 1))


def transform32(value, table, inverse):
    parts = four([tuple(x[8 * q : 8 * q + 8] for x in value) for q in range(4)], inverse)
    parts = [parts[0]] + [turned(parts[p], tuple(t[p - 1] for t in table), inverse) for p in (1, 2, 3)]
    value = stacked(parts)
    parts = four([tuple(x[:, 2 * q : 2 * q + 2] for x in value) for q in range(4)], inverse)
    sums, gaps = [], []
    for p, part in enumerate(parts):
        even, odd = tuple(x[:, 0] for x in part), tuple(x[:, 1] for x in part)
        if p == 2:
            odd = (-odd[1], odd[0]) if inverse else (odd[1], -odd[0])
        elif p:
            odd = turned(odd, scalar_turn(p, 8), inverse)
        sums.append(tuple(x + y for x, y in zip(even, odd)))
        gaps.append(tuple(x - y for x, y in zip(even, odd)))
    both = stacked(sums + gaps)
    return tuple(x.reshape((32,) + x.shape[2:]) for x in both)


def paired(first, second):
    low = iota(first.shape, first.ndim - 2) < PAIR
    first_moved = jnp.roll(first, PAIR, axis=first.ndim - 2)
    second_moved = jnp.roll(second, PAIR, axis=second.ndim - 2)
    return jnp.where(low, first, second_moved), jnp.where(low, first_moved, second)


def kernel(
    sizes, query_hbm, key_hbm, value_hbm, taps_hbm, filter_hbm, lane_hbm, counts_hbm, skip_hbm,
    out_ref,
    query_ref, key_ref, value_ref, taps_ref, filter_ref, lane_ref, counts_ref, skip_ref,
    edge_ref, border_ref, window_ref, kept_ref, skipped_ref, twist_ref, twiddle_ref, small_ref, spec_ref, start_ref,
    send_h, send_g, send_y, recv_h, recv_g, recv_y, mid_send, mid_recv,
    load_sem, far_send, far_recv, mid_send_sem, mid_recv_sem, edge_sem,
):
    outer_count, inner_count = sizes
    blocks = outer_count * inner_count
    total = blocks * LENGTH
    fine = 2 * inner_count
    outer_pos, inner_pos = lax.axis_index("outer"), lax.axis_index("inner")
    block_pos = outer_pos * inner_count + inner_pos
    side = 1 - 2 * lax.rem(inner_pos, 2)

    def block_id(pos):
        return {"outer": pos // inner_count, "inner": lax.rem(pos, inner_count)}

    following = block_id(lax.rem(block_pos + 1, blocks))
    preceding = block_id(lax.rem(block_pos + blocks - 1, blocks))

    def order(count):
        return sorted(range(1, count), key=lambda offset: -min(offset, count - offset))

    loads = [
        pltpu.make_async_copy(source, target, load_sem.at[number])
        for number, (source, target) in enumerate(
            [
                (value_hbm, value_ref), (filter_hbm, filter_ref), (taps_hbm, taps_ref),
                (key_hbm, key_ref), (query_hbm, query_ref), (lane_hbm, lane_ref),
                (counts_hbm, counts_ref), (skip_hbm, skip_ref),
            ]
        )
    ]
    for load in loads:
        load.start()

    barrier = pltpu.get_barrier_semaphore()

    def greet(device):
        pl.semaphore_signal(barrier, inc=1, device_id=device, device_id_type=MESH)

    for offset in order(outer_count):
        greet({"outer": lax.rem(outer_pos + offset, outer_count)})
    for offset in order(inner_count):
        greet({"inner": lax.rem(inner_pos + offset, inner_count)})
    greet(following)
    greet(preceding)

    def to_sets(value):
        parts = [value[:, LANES * n : LANES * (n + 1)].reshape(outer_count // 2, SUB, LANES) for n in (0, 1)]
        both = jnp.stack(paired(*parts), axis=1)
        return both.reshape(outer_count, SUB, LANES).astype(bf16)

    def arrived(ref, sem):
        pltpu.make_async_copy(ref, ref, sem).wait()

    def sent(ref, count, sem):
        part = ref.at[pl.ds(0, count)]
        pltpu.make_async_copy(part, part, sem).wait()

    def to_outer(send_ref, recv_ref, stream):
        for offset in order(outer_count):
            target = lax.rem(outer_pos + outer_count + side * offset, outer_count)
            pltpu.make_async_remote_copy(
                src_ref=send_ref.at[target], dst_ref=recv_ref.at[outer_pos],
                send_sem=far_send.at[stream], recv_sem=far_recv.at[stream],
                device_id={"outer": target}, device_id_type=MESH,
            ).start()
        pltpu.make_async_copy(send_ref.at[outer_pos], recv_ref.at[outer_pos], far_recv.at[stream]).start()

    loads[1].wait()
    send_h[...] = to_sets(filter_ref[...])
    loads[0].wait()
    window_ref[LANES:, :] = jnp.transpose(value_ref[...].astype(f32))
    border_ref[...] = window_ref[LENGTH:, :].astype(bf16)

    pl.semaphore_wait(barrier, outer_count + inner_count)
    edge = pltpu.make_async_remote_copy(
        src_ref=border_ref, dst_ref=edge_ref,
        send_sem=edge_sem.at[0], recv_sem=edge_sem.at[1],
        device_id=following, device_id_type=MESH,
    )

    edge.start()
    to_outer(send_h, recv_h, 0)

    loads[2].wait()
    loads[6].wait()
    lane = iota((1, LANES), 1)
    counts = jnp.zeros((1, LANES), jnp.int32)
    first_group = lax.axis_index("chan") * (CHANNELS // GROUP_CH)
    for group in range(CHANNELS // GROUP_CH):
        counts = jnp.where(lane // GROUP_CH == group, counts_ref[first_group + group], counts)
    live = iota((LANES, CHANNELS), 0) < counts
    kept_ref[...] = jnp.where(live, jnp.transpose(taps_ref[...]), 0.0)

    groups = LANES // SUB

    def tap(residue, step):
        return kept_ref[pl.ds(residue + SUB * step, 1), :]

    def short_late(residue, acc):
        rows = SUB * (2 * groups - 1)
        block = window_ref[pl.ds(LANES + SUB - residue, rows), :]
        for step in range(groups):
            start = SUB * (groups - 1 - step)
            acc = acc + tap(residue, step) * block[start : start + LANES]
        return acc

    def short_early(first, pairs):
        def one(residue, acc):
            acc = list(acc)
            block = window_ref[pl.ds(first - residue, LANES), :]
            for step in range(groups):
                weight = tap(residue, step)
                for place, source in pairs(step):
                    acc[place] = acc[place] + weight * block[SUB * source : SUB * (source + 1)]
            return tuple(acc)

        return one

    def own_pairs(step):
        return [(place, place - step - 1) for place in range(step + 1, groups)]

    def edge_pairs(step):
        return [(place, groups - 1 + place - step) for place in range(step + 1)]

    own_late = jnp.transpose(lax.fori_loop(0, SUB, short_late, jnp.zeros((LANES, CHANNELS), f32)))
    early = tuple(jnp.zeros((SUB, CHANNELS), f32) for _ in range(groups))
    early = lax.fori_loop(0, SUB, short_early(LANES + SUB, own_pairs), early)

    loads[3].wait()

    edge.wait_recv()
    before = edge_ref[...].astype(f32)
    window_ref[:LANES, :] = jnp.where(block_pos == 0, jnp.zeros_like(before), before)

    early = lax.fori_loop(0, SUB, short_early(SUB, edge_pairs), early)
    short_out = jnp.transpose(jnp.concatenate(early, axis=0))
    gated = key_ref[...].astype(f32) * jnp.concatenate([short_out, own_late], axis=1)
    send_g[...] = to_sets(gated)
    to_outer(send_g, recv_g, 1)

    loads[7].wait()
    skip_eye = iota((CHANNELS, CHANNELS), 0) == iota((CHANNELS, CHANNELS), 1)
    skip_col = jnp.sum(jnp.where(skip_eye, skip_ref[...], 0.0), axis=1, keepdims=True)
    skipped_ref[...] = skip_col * gated
    loads[4].wait()
    loads[5].wait()

    shape = (fine, SUB, LANES)
    lead, near = iota(shape, 0), iota(shape, 2)
    freq = 4 * (2 * inner_pos + iota(shape, 1) // PAIR) + 1
    small_shape = (24, SUB, LANES)
    small_turn = (iota(small_shape, 0) // 8 + 1) * (iota(small_shape, 0) & 7)
    for number, shift in ((0, 0), (1, 3)):
        start_ref[number] = cos_turns(lead + shift * outer_count, 4 * outer_count)
        small_ref[number] = cos_turns(small_turn + shift * 8, 32)
        twist_ref[number] = cos_turns(freq * lead + shift * outer_count * fine, 4 * outer_count * fine)
        twiddle_ref[number] = cos_turns((freq + 4 * outer_count * lead) * near + shift * total, 4 * total)

    def pair(ref):
        return ref[0], ref[1]

    def small():
        return tuple(small_ref[number].reshape(3, 8, SUB, LANES) for number in (0, 1))

    def exchange_inner(stream):
        for offset in order(inner_count):
            peer = lax.rem(inner_pos + inner_count + side * offset, inner_count)
            pltpu.make_async_remote_copy(
                src_ref=mid_send.at[stream, peer], dst_ref=mid_recv.at[stream, inner_pos],
                send_sem=mid_send_sem.at[stream], recv_sem=mid_recv_sem.at[stream],
                device_id={"inner": peer}, device_id_type=MESH,
            ).start()
        pltpu.make_async_copy(
            mid_send.at[stream, inner_pos], mid_recv.at[stream, inner_pos], mid_recv_sem.at[stream]
        ).start()

    def mid_message(halves):
        both = jnp.stack([halves[0][0], halves[0][1], halves[1][0], halves[1][1]], axis=1)
        return both.reshape(inner_count, 4 * SUB, LANES).astype(bf16)

    def coarse_forward(recv_ref, stream):
        arrived(recv_ref, far_recv.at[stream])
        value = recv_ref[...].astype(f32)
        value = transform32((value * start_ref[0], -value * start_ref[1]), small(), False)
        parts = [x.reshape(inner_count, 2, SUB, LANES) for x in value]
        real, imag = [paired(x[:, 0], x[:, 1]) for x in parts]
        mid_send[stream] = mid_message([(real[0], imag[0]), (real[1], imag[1])])
        exchange_inner(stream)

    def fine_forward(stream):
        arrived(mid_recv.at[stream], mid_recv_sem.at[stream])
        both = mid_recv[stream].astype(f32).reshape(fine, 2, SUB, LANES)
        value = transform32(turned((both[:, 0], both[:, 1]), pair(twist_ref)), small(), False)
        value = turned(value, pair(twiddle_ref))
        block = jnp.concatenate([x.reshape(fine * SUB, LANES) for x in value], axis=1)
        high, low = split(block)
        return dot(high, lane_ref[0]) + dot(low, lane_ref[0]) + dot(high, lane_ref[1])

    def halves(spec):
        return spec[:, :LANES], spec[:, LANES:]

    coarse_forward(recv_h, 0)
    coarse_forward(recv_g, 1)
    spec_ref[...] = fine_forward(0) * (1.0 / total)
    (ar, ai), (br, bi) = halves(spec_ref[...]), halves(fine_forward(1))
    high, low = split(jnp.concatenate([ar * br - ai * bi, ar * bi + ai * br], axis=1))
    block = dot(high, lane_ref[2]) + dot(low, lane_ref[2]) + dot(high, lane_ref[3])
    value = tuple(x.reshape(fine, SUB, LANES) for x in halves(block))
    value = transform32(turned(value, pair(twiddle_ref), True), small(), True)
    value = tuple(x.reshape(inner_count, 2, SUB, LANES) for x in turned(value, pair(twist_ref), True))
    mid_send[2] = mid_message([(value[0][:, n], value[1][:, n]) for n in (0, 1)])
    exchange_inner(2)

    arrived(mid_recv.at[2], mid_recv_sem.at[2])
    both = mid_recv[2].astype(f32).reshape(inner_count, 2, 2, SUB, LANES)
    parts = [jnp.stack(paired(both[:, 0, n], both[:, 1, n]), axis=1) for n in (0, 1)]
    real, imag = transform32(tuple(x.reshape(outer_count, SUB, LANES) for x in parts), small(), True)
    send_y[...] = (real * start_ref[0] - imag * start_ref[1]).astype(bf16)
    to_outer(send_y, recv_y, 2)

    arrived(recv_y, far_recv.at[2])
    sets = recv_y[...].astype(f32).reshape(outer_count // 2, 2, SUB, LANES)
    for n, long_out in enumerate(paired(sets[:, 0], sets[:, 1])):
        span = pl.ds(LANES * n, LANES)
        long_out = long_out.reshape(CHANNELS, LANES)
        out_ref[:, span] = (query_ref[:, span].astype(f32) * (long_out + skipped_ref[:, span])).astype(bf16)

    edge.wait_send()
    for stream, send_ref in enumerate((send_h, send_g, send_y)):
        sent(send_ref, outer_count - 1, far_send.at[stream])
        sent(mid_send.at[stream], inner_count - 1, mid_send_sem.at[stream])


def shards(sizes, query_in, key_in, value_in, short_filter, tap_counts, long_filter, skip_gain):
    outer_count, inner_count = sizes
    lane_all = lane_tables()
    sets = (outer_count, SUB, LANES)
    fine = (2 * inner_count, SUB, LANES)
    anywhere = pl.BlockSpec(memory_space=pl.ANY)
    return pl.pallas_call(
        functools.partial(kernel, sizes),
        out_shape=pltpu.VMEM((CHANNELS, LENGTH), bf16),
        in_specs=[anywhere] * 8,
        out_specs=pl.BlockSpec(memory_space=pltpu.VMEM),
        scratch_shapes=[
            pltpu.VMEM((CHANNELS, LENGTH), bf16),
            pltpu.VMEM((CHANNELS, LENGTH), bf16),
            pltpu.VMEM((CHANNELS, LENGTH), bf16),
            pltpu.VMEM((CHANNELS, LANES), f32),
            pltpu.VMEM((CHANNELS, LENGTH), f32),
            pltpu.VMEM(lane_all.shape, bf16),
            pltpu.SMEM(tap_counts.shape, jnp.int32),
            pltpu.VMEM((1, CHANNELS), f32),
            pltpu.VMEM((LANES, CHANNELS), bf16),
            pltpu.VMEM((LANES, CHANNELS), bf16),
            pltpu.VMEM((LANES + LENGTH, CHANNELS), f32),
            pltpu.VMEM((LANES, CHANNELS), f32),
            pltpu.VMEM((CHANNELS, LENGTH), f32),
            pltpu.VMEM((2, *fine), f32),
            pltpu.VMEM((2, *fine), f32),
            pltpu.VMEM((2, 24, SUB, LANES), f32),
            pltpu.VMEM((fine[0] * SUB, 2 * LANES), f32),
            pltpu.VMEM((2, *fine), f32),
            *[pltpu.VMEM(sets, bf16)] * 6,
            pltpu.VMEM((3, inner_count, 4 * SUB, LANES), bf16),
            pltpu.VMEM((3, inner_count, 4 * SUB, LANES), bf16),
            pltpu.SemaphoreType.DMA((8,)),
            pltpu.SemaphoreType.DMA((3,)),
            pltpu.SemaphoreType.DMA((3,)),
            pltpu.SemaphoreType.DMA((3,)),
            pltpu.SemaphoreType.DMA((3,)),
            pltpu.SemaphoreType.DMA((2,)),
        ],
        compiler_params=pltpu.CompilerParams(collective_id=0, has_side_effects=True),
    )(
        query_in, key_in, value_in, short_filter, long_filter,
        jnp.asarray(lane_all), tap_counts, skip_gain.reshape(1, CHANNELS),
    )


def solution(mesh):
    placed = (
        P("chan", ("outer", "inner")),
        P("chan", ("outer", "inner")),
        P("chan", ("outer", "inner")),
        P("chan", None),
        P(),
        P("chan", ("outer", "inner")),
        P("chan"),
    )
    sizes = (mesh.shape["outer"], mesh.shape["inner"])
    return jax.shard_map(
        functools.partial(shards, sizes),
        mesh=mesh,
        in_specs=placed,
        out_specs=P("chan", ("outer", "inner")),
        check_vma=False,
    )
```
